32 devices in a mesh: cases: 2 (over y), nodes: 4 (over z), fsdp: 2 (over x), rep: 2 (over core).
Axes of the slice: x: 2, y: 2, z: 4, core: 2. Of those that a mesh axis runs over, the one named last changes fastest.
Arguments:
- features: bfloat16 [8, 1024, 512], P(('cases', 'fsdp', 'rep'), 'nodes'), parts along dimension 0
- cotangent: bfloat16 [8, 1024, 512], P(('cases', 'fsdp', 'rep'), 'nodes'), parts along dimension 0
- weights: bfloat16 [2, 2, 512, 512], P(None, None, 'fsdp'), may hold values from -0.25 to 0.25
- gains: float32 [2, 512], replicated, may hold values from 0.25 to 1.75
- tile_pairs: int32 [4, 2, 12], P('nodes'), may hold values from 0 to 3, as said below
- halo_send: int32 [4, 2, 1], P('nodes'), may hold values from 0 to 1, as said below
- entry_counts: int32 [4], P('nodes'), may hold values from 2 to 12, as said below
- tile_values: bfloat16 [4, 12, 128, 128], P('nodes'), may hold values from -0.375 to 0.375
Outputs:
- output: bfloat16 [8, 1024, 512], P(('cases', 'fsdp', 'rep'), 'nodes'), parts along dimension 0
- weight_grads: float32 [512, 4, 2, 512], P('fsdp', 'cases'), parts along dimension 1
- gain_grads: float32 [4, 512], P('cases'), parts along dimension 0
The draws below stay inside these ranges and needn't reach their ends.
There are 2 independent parts, one for each index of `cases`. The reference program is written for one: setup_inputs(seed, part) draws one part's arguments, and reference() takes and returns one part's arrays. A program takes and returns all parts, laid end to end along the dimension named above; an argument that names none is the same for every part. Nothing has to cross between parts.
Inputs may be any that keep to these rules, and one draw needn't show every extreme that they name: `tile_pairs`: entries 0 to 1 of every partition name the column tiles 2 to 3 in order; row tiles are below 2. Each list halo_send[q, k] holds 1 distinct tiles. `entry_counts`: exactly one partition has all 12 entries live; every other one at most 6.
All inputs are finite; a program needn't handle non-finite values.
Results may differ from the reference program's by a relative error of at most 0.014.
Values may be sent and summed in bfloat16 or wider, within the bound.
No kernel may reach another device: no remote copies, remote signals or barrier semaphores. Data moves between devices by JAX's collectives and lax.ppermute only.
A program may use at most 64 MiB of HBM per device.

```python
import math
import jax
import jax.numpy as jnp
from jax import lax

D = 512
TILE = 128
TILES_DEV = 2
HALO_TILES = 1
ENTRIES_DEV = 12
LAYERS = 2
PARTITIONS = 4
NTILES = 8
NODES = 1024
SAMPLES = 4
N_NODES = 4


def draw_features(key, part):
    keys = jax.random.split(key, 3)
    spread_log = math.log(10.0)
    row_scale = jnp.exp(jax.random.uniform(keys[0], (SAMPLES, NODES, 1), jnp.float32) * spread_log) / math.sqrt(10.0)
    col_scale = jnp.exp(jax.random.uniform(keys[1], (1, 1, D), jnp.float32) * spread_log) / math.sqrt(10.0)
    values = jax.random.truncated_normal(keys[2], -4.0, 4.0, (SAMPLES, NODES, D), jnp.float32) * row_scale * col_scale
    return values.astype(jnp.bfloat16)


def draw_cotangent(key, part):
    keys = jax.random.split(key, 1)
    node_pos = jnp.arange(NODES, dtype=jnp.float32)[None, :, None] / NODES
    rising = (1.0 + 2.0 * node_pos) / math.sqrt(SAMPLES * NODES)
    values = jax.random.truncated_normal(keys[0], -4.0, 4.0, (SAMPLES, NODES, D), jnp.float32) * rising
    return values.astype(jnp.bfloat16)


def draw_tile_pairs(key, part):
    keys = jax.random.split(key, 2)
    row_ids = jax.random.randint(keys[0], (N_NODES, ENTRIES_DEV), 0, TILES_DEV)
    col_ids = jax.random.randint(keys[1], (N_NODES, ENTRIES_DEV), 0, TILES_DEV + 2 * HALO_TILES)
    fixed_cols = TILES_DEV + jnp.arange(2 * HALO_TILES)
    col_ids = col_ids.at[:, :2 * HALO_TILES].set(jnp.broadcast_to(fixed_cols[None, :], (N_NODES, 2 * HALO_TILES)))
    return jnp.stack([row_ids, col_ids], axis=1).astype(jnp.int32)


def draw_halo_send(key, part):
    keys = jax.random.split(key, N_NODES * 2)
    picked = jax.vmap(lambda single: jax.random.permutation(single, TILES_DEV)[:HALO_TILES])(keys)
    return picked.reshape(N_NODES, 2, HALO_TILES).astype(jnp.int32)


def draw_entry_counts(key, part):
    keys = jax.random.split(key, 2)
    counts = jax.random.randint(keys[0], (N_NODES,), 2 * HALO_TILES, ENTRIES_DEV // 2 + 1)
    busiest = jax.random.randint(keys[1], (), 0, N_NODES)
    return jnp.where(jnp.arange(N_NODES) == busiest, ENTRIES_DEV, counts).astype(jnp.int32)


def block_levels(stream_key, shape, cuts, least, top_value):
    level = 1.0
    for dim, shards_of in cuts:
        heights = jax.random.uniform(jax.random.fold_in(jax.random.fold_in(stream_key, 6), dim), (shards_of,), jnp.float32, least / len(cuts), top_value / len(cuts))
        level = level * jnp.repeat(jnp.exp(heights), shape[dim] // shards_of).reshape((-1,) + (1,) * (len(shape) - 1 - dim))
    return level


def centred(key, dims, width, bound, pieces=(), kind=jnp.bfloat16):
    factor_of = block_levels(key, dims, pieces, -0.22, 0.18) if pieces else 1.0
    values = jax.random.normal(key, dims, jnp.float32) * width * factor_of
    return jnp.minimum(jnp.maximum(values, -bound), bound).astype(kind)


def setup_inputs(seed: int = 0, part: int = 0) -> dict:
    key_list = jax.random.split(jax.random.key(seed), 9)
    part_keys = jax.random.split(jax.random.fold_in(key_list[8], part), 9)
    features = draw_features(jax.random.fold_in(jax.random.fold_in(key_list[8], part), 71), part)
    cotangent = draw_cotangent(jax.random.fold_in(jax.random.fold_in(key_list[8], part), 71), part)
    weights = centred(key_list[2], (LAYERS, 2, D, D), D ** -0.5, 0.25, ((2, 2),))
    gains = jnp.clip(1.0 + 0.15 * jax.random.normal(key_list[3], (LAYERS, D), jnp.float32), 0.25, 1.75)
    tile_pairs = draw_tile_pairs(jax.random.fold_in(key_list[8], 71), part)
    halo_send = draw_halo_send(jax.random.fold_in(key_list[8], 71), part)
    entry_counts = draw_entry_counts(jax.random.fold_in(key_list[8], 71), part)
    tile_values = centred(key_list[7], (PARTITIONS, ENTRIES_DEV, TILE, TILE), (2 * TILE) ** -0.5, 0.375, ((0, 4),))
    return dict(features=features, cotangent=cotangent, weights=weights, gains=gains, tile_pairs=tile_pairs, halo_send=halo_send, entry_counts=entry_counts, tile_values=tile_values)


EPSILON = 1e-05

def silu_slope(values):
    sigmoid_part = jax.nn.sigmoid(values)
    return sigmoid_part * (1.0 + values * (1.0 - sigmoid_part))

def column_table(halo_send):
    part_ids = jnp.arange(PARTITIONS, dtype=jnp.int32)
    local_ids = part_ids[:, None] * TILES_DEV + jnp.arange(TILES_DEV, dtype=jnp.int32)[None, :]
    lower_ids = jnp.roll(halo_send[:, 1, :], 1, axis=0) + (part_ids[:, None] - 1) * TILES_DEV
    upper_ids = jnp.roll(halo_send[:, 0, :], -1, axis=0) + (part_ids[:, None] + 1) * TILES_DEV
    table = jnp.concatenate([local_ids, lower_ids, upper_ids], axis=1).astype(jnp.int32)
    valid = jnp.concatenate([jnp.ones((PARTITIONS, TILES_DEV), dtype=bool), jnp.broadcast_to((part_ids > 0)[:, None], (PARTITIONS, HALO_TILES)), jnp.broadcast_to((part_ids < PARTITIONS - 1)[:, None], (PARTITIONS, HALO_TILES))], axis=1)
    table = jnp.where(valid, table, 0).astype(jnp.int32)
    return (table, valid)

def sweep_tiles(sources, values_flat, target_ids, source_ids, live, transposed):

    def step(summed, entry):
        tile_matrix, target_id, source_id, alive = entry
        source_tile = lax.dynamic_index_in_dim(sources, source_id, 1, keepdims=False).astype(jnp.float32)
        wide_tile = tile_matrix.astype(jnp.float32)
        if transposed:
            term = jnp.einsum('ij,sid->sjd', wide_tile, source_tile)
        else:
            term = jnp.einsum('ij,sjd->sid', wide_tile, source_tile)
        term = jnp.where(alive, term, jnp.zeros_like(term))
        present = lax.dynamic_index_in_dim(summed, target_id, 1, keepdims=True)
        summed = lax.dynamic_update_index_in_dim(summed, present + term[:, None], target_id, 1)
        return (summed, None)
    start = jnp.zeros((SAMPLES, NTILES, TILE, D), jnp.float32)
    summed, unused = lax.scan(step, start, (values_flat, target_ids, source_ids, live))
    return summed

def reference(features, cotangent, weights, gains, tile_pairs, halo_send, entry_counts, tile_values):
    rows_all = SAMPLES * NODES
    table, valid = column_table(halo_send)
    part_ids = jnp.arange(PARTITIONS, dtype=jnp.int32)
    entry_ids = jnp.arange(ENTRIES_DEV, dtype=jnp.int32)
    local_cols = tile_pairs[:, 1, :].astype(jnp.int32)
    rows_global = (part_ids[:, None] * TILES_DEV + tile_pairs[:, 0, :]).reshape(-1).astype(jnp.int32)
    cols_global = jnp.take_along_axis(table, local_cols, axis=1).reshape(-1).astype(jnp.int32)
    live = ((entry_ids[None, :] < entry_counts[:, None]) & jnp.take_along_axis(valid, local_cols, axis=1)).reshape(-1)
    values_flat = tile_values.reshape(PARTITIONS * ENTRIES_DEV, TILE, TILE)
    current = features
    saved = []
    for layer_id in range(LAYERS):
        widened = current.astype(jnp.float32)
        inv_rms = lax.rsqrt(lax.optimization_barrier(jnp.mean(widened * widened, axis=-1, keepdims=True)) + EPSILON)
        normed = (widened * inv_rms * gains[layer_id]).astype(jnp.bfloat16)
        flat_normed = normed.reshape(rows_all, D)
        direct = jnp.dot(flat_normed, weights[layer_id, 0], preferred_element_type=jnp.float32)
        messages = jnp.dot(flat_normed, weights[layer_id, 1], preferred_element_type=jnp.float32).astype(jnp.bfloat16)
        summed = sweep_tiles(messages.reshape(SAMPLES, NTILES, TILE, D), values_flat, rows_global, cols_global, live, False)
        before = direct.reshape(SAMPLES, NODES, D) + summed.reshape(SAMPLES, NODES, D)
        saved.append((widened, inv_rms, flat_normed, before))
        current = (widened + jax.nn.silu(before)).astype(jnp.bfloat16)
    output = current
    upstream = cotangent.astype(jnp.float32)
    grad_blocks = [None] * LAYERS
    gain_rows = [None] * LAYERS
    for layer_id in reversed(range(LAYERS)):
        widened, inv_rms, flat_normed, before = saved[layer_id]
        slope = (upstream * silu_slope(before)).astype(jnp.bfloat16)
        returned = sweep_tiles(slope.reshape(SAMPLES, NTILES, TILE, D), values_flat, cols_global, rows_global, live, True)
        back_messages = returned.astype(jnp.bfloat16).reshape(rows_all, D)
        flat_slope = slope.reshape(rows_all, D)
        dnormed = jnp.dot(flat_slope, weights[layer_id, 0].T, preferred_element_type=jnp.float32) + jnp.dot(back_messages, weights[layer_id, 1].T, preferred_element_type=jnp.float32)
        grad_self = jnp.dot(flat_normed.T, flat_slope, preferred_element_type=jnp.float32)
        grad_other = jnp.dot(flat_normed.T, back_messages, preferred_element_type=jnp.float32)
        grad_blocks[layer_id] = jnp.stack([grad_self, grad_other])
        dnormed = dnormed.reshape(SAMPLES, NODES, D)
        gain_rows[layer_id] = lax.optimization_barrier(jnp.sum(dnormed * widened * inv_rms, axis=(0, 1)))
        if layer_id > 0:
            scaled = dnormed * gains[layer_id]
            mean_part = lax.optimization_barrier(jnp.mean(scaled * widened, axis=-1, keepdims=True))
            upstream = upstream + inv_rms * scaled - widened * (inv_rms * inv_rms * inv_rms) * mean_part
    weight_grads = jnp.transpose(jnp.stack(grad_blocks), (2, 0, 1, 3))
    gain_grads = jnp.stack(gain_rows)
    return (output, weight_grads, gain_grads)
```

```python
import functools

import jax
import jax.numpy as jnp
from jax import lax
from jax.experimental import pallas as pl
from jax.experimental.pallas import tpu as pltpu
from jax.sharding import PartitionSpec as P

EPSILON = 1e-05
BF16 = jnp.bfloat16
F32 = jnp.float32
DIRECT_NODES = 4


VMEM = pl.BlockSpec(memory_space=pltpu.VMEM)
SMEM = pl.BlockSpec(memory_space=pltpu.SMEM)


def call(kernel, outs, in_specs, scratch=()):
    return pl.pallas_call(
        kernel,
        out_shape=tuple(jax.ShapeDtypeStruct(s, d) for s, d in outs),
        in_specs=in_specs,
        out_specs=tuple(VMEM for _ in outs),
        scratch_shapes=list(scratch),
    )


def mm(a, b):
    return lax.dot_general(a, b, (((1,), (0,)), ((), ())), preferred_element_type=F32)


def mm_t(a, b):
    return lax.dot_general(a, b, (((1,), (1,)), ((), ())), preferred_element_type=F32)


def inverse_rms(wide):
    return lax.rsqrt(jnp.mean(wide * wide, axis=-1, keepdims=True) + EPSILON)


def sigmoid(v):
    return 1.0 / (1.0 + jnp.exp(-v))


def adjacency_kernel(pairs, count, values, a_ref, at_ref, acc):
    entries, tile = values.shape[0], values.shape[1]
    tiles_ext = acc.shape[0]
    tiles = acc.shape[1] // tile
    acc[...] = jnp.zeros_like(acc)

    def step(e, carry):
        row = pairs[0, e]
        col = pairs[1, e]
        at = pl.ds(pl.multiple_of(row * tile, tile), tile)
        acc[col, at, :] = acc[col, at, :] + values[e].astype(F32)
        return carry

    lax.fori_loop(0, count[0], step, 0)
    for c in range(tiles_ext):
        block = acc[c]
        a_ref[:, c * tile : (c + 1) * tile] = block.astype(BF16)
        at_ref[c * tile : (c + 1) * tile, :] = block.T.astype(BF16)


def normed_of(x_bf16, gain):
    wide = x_bf16.astype(F32)
    inv = inverse_rms(wide)
    return wide, inv, (wide * inv * gain).astype(BF16)


def assemble(where, own, mine, other, full):
    rows = own.shape[1]
    part = mine.shape[2]
    full[:, pl.ds(pl.multiple_of(where[0], part), rows), :] = own[...]
    for k in range(mine.shape[0]):
        full[:, pl.ds(pl.multiple_of(where[1 + 2 * k], part), part), :] = mine[k]
        full[:, pl.ds(pl.multiple_of(where[2 + 2 * k], part), part), :] = other[k]


def first_layer_kernel(where, sends, x, low, high, own, mine, other, a, gains,
                       full, slope_factor, normed, nxt, send_low, send_high, *, layer, tile):
    samples, rows, _ = x.shape
    rim = low.shape[1]
    assemble(where, own, mine, other, full)
    gain = gains[layer : layer + 1, :]
    w_self = full[0]
    w_other = full[1]
    for s in range(samples):
        wide, _, mine_n = normed_of(x[s], gain)
        _, _, low_n = normed_of(low[s], gain)
        _, _, high_n = normed_of(high[s], gain)
        normed[s, :rows] = mine_n
        normed[s, rows : rows + rim] = low_n
        normed[s, rows + rim :] = high_n
        messages = mm(normed[s], w_other).astype(BF16)
        before = mm(mine_n, w_self) + mm(a[...], messages)
        sig = sigmoid(before)
        slope_factor[s] = sig * (1.0 + before * (1.0 - sig))
        nxt[s] = (wide + before * sig).astype(BF16)
        for j in range(rim // tile):
            send_low[s, j * tile : (j + 1) * tile] = nxt[
                s, pl.ds(pl.multiple_of(sends[0, j] * tile, tile), tile), :]
            send_high[s, j * tile : (j + 1) * tile] = nxt[
                s, pl.ds(pl.multiple_of(sends[1, j] * tile, tile), tile), :]


def own_part_kernel(where, x, own, mine, other, a, gains, full, partial, normed, *, layer):
    samples, rows, _ = x.shape
    assemble(where, own, mine, other, full)
    gain = gains[layer : layer + 1, :]
    for s in range(samples):
        _, _, mine_n = normed_of(x[s], gain)
        normed[s] = mine_n
        messages = mm(mine_n, full[1]).astype(BF16)
        partial[s] = mm(mine_n, full[0]) + mm(a[:, :rows], messages)


def last_layer_kernel(x, low, high, partial, cot, full, a, at, gains,
                      out, slope, returned, border_low, border_high, halo_normed, *, layer):
    samples, rows, _ = x.shape
    rim = low.shape[1]
    gain = gains[layer : layer + 1, :]
    for s in range(samples):
        _, _, low_n = normed_of(low[s], gain)
        _, _, high_n = normed_of(high[s], gain)
        halo_normed[s, :rim] = low_n
        halo_normed[s, rim:] = high_n
        messages = mm(halo_normed[s], full[1]).astype(BF16)
        before = partial[s] + mm(a[:, rows:], messages)
        sig = sigmoid(before)
        out[s] = (x[s].astype(F32) + before * sig).astype(BF16)
        slope[s] = (cot[s].astype(F32) * (sig * (1.0 + before * (1.0 - sig)))).astype(BF16)
        back = mm(at[...], slope[s])
        returned[s] = back[:rows]
        border_low[s] = back[rows : rows + rim].astype(BF16)
        border_high[s] = back[rows + rim :].astype(BF16)


def middle_kernel(x, low, high, partial, full, a, gains, slope_factor, nxt, halo_normed, *, layer):
    samples, rows, _ = x.shape
    rim = low.shape[1]
    gain = gains[layer : layer + 1, :]
    for s in range(samples):
        _, _, low_n = normed_of(low[s], gain)
        _, _, high_n = normed_of(high[s], gain)
        halo_normed[s, :rim] = low_n
        halo_normed[s, rim:] = high_n
        messages = mm(halo_normed[s], full[1]).astype(BF16)
        before = partial[s] + mm(a[:, rows:], messages)
        sig = sigmoid(before)
        slope_factor[s] = sig * (1.0 + before * (1.0 - sig))
        nxt[s] = (x[s].astype(F32) + before * sig).astype(BF16)


def grads_pair(place, normed_t_list, slope, back, keep, send):
    samples, rows, _ = slope.shape
    self_grad = None
    other_grad = None
    for s in range(samples):
        own_t, halo_t = normed_t_list[s]
        g_self = mm(own_t, slope[s])
        g_other = mm(own_t, back[s, :rows]) + mm(halo_t, back[s, rows:])
        self_grad = g_self if self_grad is None else self_grad + g_self
        other_grad = g_other if other_grad is None else other_grad + g_other

    @pl.when(place == 0)
    def _():
        keep[...] = self_grad
        send[...] = other_grad.astype(BF16)

    @pl.when(place != 0)
    def _():
        keep[...] = other_grad
        send[...] = self_grad.astype(BF16)


def window_kernel(place, normed, halo_normed, slope, returned, border_low, border_high, full,
                  keep, send, dn_part, back):
    samples, rows, _ = slope.shape
    rim = border_low.shape[1]
    lists = []
    for s in range(samples):
        back[s, :rows] = returned[s].astype(BF16)
        back[s, rows : rows + rim] = border_low[s]
        back[s, rows + rim :] = border_high[s]
        lists.append((normed[s].T, halo_normed[s].T))
        dn_part[s] = mm_t(slope[s], full[0])
    grads_pair(place[0], lists, slope, back, keep, send)


def backward_kernel(place, sends, x, cot, slope_factor, returned, from_low, from_high, dn_part,
                    full, at, gains, normed_t, gain_out, slope, back, keep, send, ret, *, layer, tile):
    samples, rows, _ = x.shape
    rim = from_low.shape[1]
    gain = gains[layer : layer + 1, :]
    total = None
    lists = []
    for s in range(samples):
        ret[...] = returned[s]
        for j in range(rim // tile):
            low_at = pl.ds(pl.multiple_of(sends[0, j] * tile, tile), tile)
            ret[low_at, :] = ret[low_at, :] + from_low[s, j * tile : (j + 1) * tile].astype(F32)
        for j in range(rim // tile):
            high_at = pl.ds(pl.multiple_of(sends[1, j] * tile, tile), tile)
            ret[high_at, :] = ret[high_at, :] + from_high[s, j * tile : (j + 1) * tile].astype(F32)
        dnormed = dn_part[s] + mm_t(ret[...].astype(BF16), full[1])
        wide = x[s].astype(F32)
        inv = inverse_rms(wide)
        unit = wide * inv
        piece = jnp.sum(dnormed * unit, axis=0, keepdims=True)
        total = piece if total is None else total + piece
        scaled = dnormed * gain
        mean_part = jnp.mean(scaled * wide, axis=-1, keepdims=True)
        upstream = cot[s].astype(F32) + inv * scaled - wide * (inv * inv * inv) * mean_part
        slope[s] = (upstream * slope_factor[s]).astype(BF16)
        back[s] = mm(at[...], slope[s]).astype(BF16)
        lists.append((normed_t[s, :, :rows], normed_t[s, :, rows:]))
    gain_out[...] = total
    grads_pair(place[0], lists, slope, back, keep, send)


def transpose_kernel(x, out):
    for s in range(x.shape[0]):
        out[s] = x[s].T


def gain_kernel(x, low, high, slope, back, full, gain_above, out):
    samples, rows, _ = x.shape
    rim = low.shape[1]
    total = None
    for s in range(samples):
        dn_self = mm_t(slope[s], full[0])
        dn_other = mm_t(back[s], full[1])
        pieces = (
            (x[s], dn_self + dn_other[:rows]),
            (low[s], dn_other[rows : rows + rim]),
            (high[s], dn_other[rows + rim :]),
        )
        for tiles, dn in pieces:
            wide = tiles.astype(F32)
            piece = jnp.sum(dn * (wide * inverse_rms(wide)), axis=0, keepdims=True)
            total = piece if total is None else total + piece
    both = jnp.concatenate([total, gain_above[...]], axis=0)
    coarse = both.astype(BF16)
    fine = (both - coarse.astype(F32)).astype(BF16)
    out[...] = jnp.zeros_like(out)
    out[0:2, :] = coarse
    out[2:4, :] = fine


def shift_pairs(count, k):
    if count & (count - 1) == 0:
        return [(i, i ^ k) for i in range(count)]
    return [(i, (i + k) % count) for i in range(count)]


def source_of(index, count, k):
    if count & (count - 1) == 0:
        return index ^ k
    return (index - k) % count


def target_of(index, count, k):
    if count & (count - 1) == 0:
        return index ^ k
    return (index + k) % count


def split_pair(value):
    coarse = value.astype(BF16)
    return coarse, (value - coarse.astype(F32)).astype(BF16)


def tree_sum(terms):
    while len(terms) > 1:
        terms = [terms[i] + terms[i + 1] if i + 1 < len(terms) else terms[i]
                 for i in range(0, len(terms), 2)]
    return terms[0]


def rows_at(array, start, size):
    return lax.dynamic_slice_in_dim(array, start, size, axis=0)


def body(features, cotangent, weights, gains, tile_pairs, halo_send, entry_counts, tile_values):
    samples, rows, width = features.shape
    layers, _, w_rows, _ = weights.shape
    tile = tile_values.shape[-1]
    tiles = rows // tile
    halo = halo_send.shape[2]
    rim = halo * tile
    ext = rows + 2 * rim
    n_nodes = lax.axis_size("nodes")
    n_fsdp = lax.axis_size("fsdp")
    n_rep = lax.axis_size("rep")
    assert n_rep == 2 and layers == 2
    fsdp_id = lax.axis_index("fsdp")
    rep_id = lax.axis_index("rep")
    node_id = lax.axis_index("nodes")
    swap = [(0, 1), (1, 0)]
    up = [(i, i + 1) for i in range(n_nodes - 1)]
    down = [(j, i) for i, j in up]
    sends = halo_send[0]
    pairs = tile_pairs[0]
    place = rep_id.astype(jnp.int32).reshape(1)
    part = w_rows // n_rep

    spots = [fsdp_id * w_rows]
    for k in range(1, n_fsdp):
        base = source_of(fsdp_id, n_fsdp, k) * w_rows
        spots += [base + rep_id * part, base + (1 - rep_id) * part]
    where = jnp.stack(spots).astype(jnp.int32)

    def fetch(layer):
        piece = lax.dynamic_slice_in_dim(weights[layer], rep_id * part, part, axis=1)
        got = [lax.ppermute(piece, "fsdp", shift_pairs(n_fsdp, k)) for k in range(1, n_fsdp)]
        return jnp.stack(got)

    fetched = [fetch(0)]

    def picked(x, side):
        got = [lax.dynamic_slice_in_dim(x, sends[side, j] * tile, tile, axis=1) for j in range(halo)]
        return got[0] if halo == 1 else jnp.concatenate(got, axis=1)

    low0 = lax.ppermute(picked(features, 1), "nodes", up)
    high0 = lax.ppermute(picked(features, 0), "nodes", down)
    fetched.append(fetch(1))
    others = [lax.ppermute(piece, "rep", swap) for piece in fetched]

    a, at = call(
        adjacency_kernel,
        [((rows, ext), BF16), ((ext, rows), BF16)],
        [SMEM, SMEM, VMEM],
        [pltpu.VMEM((tiles + 2 * halo, rows, tile), F32)],
    )(pairs, entry_counts, tile_values[0])

    act = (samples, rows, width)
    rim_shape = (samples, rim, width)
    full_shape = (2, width, width)
    full0, factor0, normed0, x1, send_low, send_high = call(
        functools.partial(first_layer_kernel, layer=0, tile=tile),
        [(full_shape, BF16), (act, F32), ((samples, ext, width), BF16), (act, BF16),
         (rim_shape, BF16), (rim_shape, BF16)],
        [SMEM, SMEM] + [VMEM] * 8,
    )(where, sends, features, low0, high0, weights[0], fetched[0], others[0], a, gains)

    low1 = lax.ppermute(send_high, "nodes", up)
    high1 = lax.ppermute(send_low, "nodes", down)
    full1, partial1, normed1 = call(
        functools.partial(own_part_kernel, layer=1),
        [(full_shape, BF16), (act, F32), (act, BF16)],
        [SMEM] + [VMEM] * 6,
    )(where, x1, weights[1], fetched[1], others[1], a, gains)
    (normed0_t,) = call(
        transpose_kernel, [((samples, width, ext), BF16)], [VMEM])(normed0)

    output, slope1, returned1, border_low, border_high, halo_normed1 = call(
        functools.partial(last_layer_kernel, layer=1),
        [(act, BF16), (act, BF16), (act, F32), (rim_shape, BF16), (rim_shape, BF16),
         ((samples, 2 * rim, width), BF16)],
        [VMEM] * 9,
    )(x1, low1, high1, partial1, cotangent, full1, a, at, gains)

    from_low = lax.ppermute(border_high, "nodes", up)
    from_high = lax.ppermute(border_low, "nodes", down)
    square = (width, width)
    keep1, give1, dn_part, _ = call(
        window_kernel,
        [(square, F32), (square, BF16), (act, F32), ((samples, ext, width), BF16)],
        [SMEM] + [VMEM] * 7,
    )(place, normed1, halo_normed1, slope1, returned1, border_low, border_high, full1)

    gain1, slope0, back0, keep0, give0 = call(
        functools.partial(backward_kernel, layer=1, tile=tile),
        [((1, width), F32), (act, BF16), ((samples, ext, width), BF16), (square, F32), (square, BF16)],
        [SMEM, SMEM] + [VMEM] * 11,
        [pltpu.VMEM((rows, width), F32)],
    )(place, sends, x1, cotangent, factor0, returned1, from_low, from_high, dn_part,
      full1, at, gains, normed0_t)

    (gain_rows,) = call(
        gain_kernel, [((16, width), BF16)], [VMEM] * 7,
    )(features, low0, high0, slope0, back0, full0, gain1)

    half = width // n_fsdp
    chunk = half // n_nodes
    direct_nodes = n_nodes <= DIRECT_NODES and chunk % 16 == 0

    def wide_gain(rows_bf16):
        return rows_bf16[0:2].astype(F32) + rows_bf16[2:4].astype(F32)

    def pack_gain(gain):
        coarse, fine = split_pair(gain)
        filler = jnp.zeros((12, width), BF16)
        return jnp.concatenate([coarse, fine, filler], axis=0)

    def reduce_layer(keep, give, gain):
        summed = keep + lax.ppermute(give, "rep", swap).astype(F32)
        if gain is not None:
            gain = wide_gain(gain) + wide_gain(lax.ppermute(gain, "rep", swap))
            gain = pack_gain(gain)
        terms = [rows_at(summed, fsdp_id * half, half)]
        gains_in = []
        for k in range(1, n_fsdp):
            payload = rows_at(summed, target_of(fsdp_id, n_fsdp, k) * half, half).astype(BF16)
            if gain is not None:
                payload = jnp.concatenate([payload, gain], axis=0)
            got = lax.ppermute(payload, "fsdp", shift_pairs(n_fsdp, k))
            terms.append(got[:half].astype(F32))
            if gain is not None:
                gains_in.append(wide_gain(got[half:]))
        summed = tree_sum(terms)
        if gain is not None:
            gain = tree_sum([wide_gain(gain)] + gains_in)
        if not direct_nodes:
            summed = lax.psum(summed, "nodes").astype(BF16)
            if gain is not None:
                gain = lax.psum(gain, "nodes")
            return summed, gain
        if gain is not None:
            gain = pack_gain(gain)
        rounded = summed.astype(BF16)
        terms = [rows_at(summed, node_id * chunk, chunk)]
        gains_in = []
        for k in range(1, n_nodes):
            payload = rows_at(rounded, target_of(node_id, n_nodes, k) * chunk, chunk)
            if gain is not None:
                payload = jnp.concatenate([payload, gain], axis=0)
            got = lax.ppermute(payload, "nodes", shift_pairs(n_nodes, k))
            terms.append(got[:chunk].astype(F32))
            if gain is not None:
                gains_in.append(wide_gain(got[chunk:]))
        mine = tree_sum(terms).astype(BF16)
        if gain is not None:
            gain = tree_sum([wide_gain(gain)] + gains_in)
        whole = jnp.zeros((half, width), BF16)
        whole = lax.dynamic_update_slice_in_dim(whole, mine, node_id * chunk, axis=0)
        for k in range(1, n_nodes):
            got = lax.ppermute(mine, "nodes", shift_pairs(n_nodes, k))
            whole = lax.dynamic_update_slice_in_dim(
                whole, got, source_of(node_id, n_nodes, k) * chunk, axis=0)
        return whole, gain

    part1, _ = reduce_layer(keep1, give1, None)
    part0, gain_grads = reduce_layer(keep0, give0, gain_rows)

    blocks = []
    for mine in (part0, part1):
        other = lax.ppermute(mine, "rep", swap)
        first = jnp.where(rep_id == 0, mine, other)
        second = jnp.where(rep_id == 0, other, mine)
        blocks.append(jnp.stack([first, second], axis=1))
    weight_grads = jnp.stack(blocks, axis=1).astype(F32)
    return output, weight_grads, gain_grads


def solution(mesh):
    placed = (
        P(("cases", "fsdp", "rep"), "nodes", None),
        P(("cases", "fsdp", "rep"), "nodes", None),
        P(None, None, "fsdp", None),
        P(),
        P("nodes", None, None),
        P("nodes", None, None),
        P("nodes"),
        P("nodes", None, None, None),
    )
    return jax.shard_map(
        body,
        mesh=mesh,
        in_specs=placed,
        out_specs=(
            P(("cases", "fsdp", "rep"), "nodes", None),
            P("fsdp", "cases", None, None),
            P("cases", None),
        ),
        check_vma=False,
    )
```
